512 devices in a mesh: tm: 16 (over z_lo, core), inp: 32 (over x, y, z_hi).
Axes of the slice: x: 4, y: 4, z: 16 (z_hi: 2, z_lo: 8; z = z_hi * 8 + z_lo), core: 2. Of those that a mesh axis runs over, the one named last changes fastest.
Arguments:
- voltage: int32 [256, 2097152], P('inp', 'tm'), may hold values from -127 to 127
- taps: float32 [4, 512], replicated, may hold values from -0.0625 to 0.0625
- chan_table: int32 [256], replicated, may hold values from 0 to 255, each once
Outputs:
- visibility: float32 [256, 128, 256], P('tm', 'inp')
- beam: float32 [128, 4096], P('inp', 'tm')
The draws below stay inside these ranges and needn't reach their ends.
Inputs may be any that keep to these rules, and one draw needn't show every extreme that they name: `chan_table`: each channel number appears once.
All inputs are finite; a program needn't handle non-finite values.
Results may differ from the reference program's by a relative error of at most 0.0016.
Values may be sent and summed in bfloat16 or wider, within the bound.
A program may use at most 64 MiB of HBM per device.

```python
import math
import jax
import jax.numpy as jnp
from jax import lax

NIN = 256
P_SIZE = 512
TAPS = 4
NCH = 128
BAND = 256
SAMPLES = 2097152


def draw_voltage(key, part):
    first, second = jax.random.split(jax.random.fold_in(key, 11))
    amplitude = jnp.minimum(jax.random.randint(first, (NIN, 1), 12, 160), 127).astype(jnp.int32)
    return jax.random.randint(second, (NIN, SAMPLES), -amplitude, amplitude + 1).astype(jnp.int32)


def normal_values(rng, extent, spread, bound, held_as=jnp.bfloat16):
    result = spread * jax.random.normal(rng, extent, jnp.float32)
    return jnp.clip(result, min=-bound, max=bound).astype(held_as)


def setup_inputs(seed: int = 0) -> dict:
    key_list = jax.random.split(jax.random.key(seed), 4)
    return {
        "voltage": draw_voltage(jax.random.fold_in(key_list[3], 71), 0),
        "taps": normal_values(key_list[1], (TAPS, P_SIZE), 0.01, 0.0625, jnp.float32),
        "chan_table": jax.random.permutation(key_list[2], BAND).astype(jnp.int32),
    }


def dft_table(chan_table):
    chosen = chan_table[:NCH].astype(jnp.int32)
    points = jnp.arange(P_SIZE, dtype=jnp.int32)
    phase = chosen[:, None] * points[None, :] % P_SIZE
    angle = phase.astype(jnp.float32) * (2.0 * math.pi / P_SIZE)
    factor = 1.0 / math.sqrt(P_SIZE)
    table = jnp.stack([jnp.cos(angle) * factor, -jnp.sin(angle) * factor], axis=1)
    return table.astype(jnp.bfloat16)

def reference(voltage, taps, chan_table):
    table = dft_table(chan_table)
    total = voltage.shape[1] // P_SIZE
    group_rows = 16

    def channelize(block):
        volts = block.astype(jnp.float32).reshape(group_rows, total, P_SIZE)
        padded = jnp.concatenate([jnp.zeros((group_rows, TAPS - 1, P_SIZE), jnp.float32), volts], axis=1)
        filtered = jnp.zeros((group_rows, total, P_SIZE), jnp.float32)
        for tap_index in range(TAPS):
            filtered = filtered + taps[tap_index] * padded[:, tap_index:tap_index + total, :]
        filtered = filtered.astype(jnp.bfloat16)
        spectra = jnp.einsum('cqp,isp->cqis', table.astype(jnp.float32), filtered.astype(jnp.float32), preferred_element_type=jnp.float32)
        return spectra.astype(jnp.bfloat16)
    blocks = voltage.reshape(NIN // group_rows, group_rows, voltage.shape[1])
    spectra = lax.map(channelize, blocks)
    spectra = jnp.transpose(spectra, (1, 2, 0, 3, 4)).reshape(NCH, 2, NIN, total)
    upper = jnp.arange(NIN, dtype=jnp.int32)[:, None] <= jnp.arange(NIN, dtype=jnp.int32)[None, :]

    def correlate(parts):
        real_in = parts[0].astype(jnp.float32)
        imag_in = parts[1].astype(jnp.float32)
        combined = jnp.concatenate([real_in, imag_in], axis=1)
        rotated = jnp.concatenate([imag_in, -real_in], axis=1)
        re_part = jnp.dot(combined, combined.T, preferred_element_type=jnp.float32)
        im_part = jnp.dot(rotated, combined.T, preferred_element_type=jnp.float32)
        packed = jnp.where(upper, re_part, im_part) / total
        power = lax.optimization_barrier(jnp.sum(parts.astype(jnp.float32) ** 2, axis=(0, 1))) / NIN
        return (packed, power)
    packed_all, beam = lax.map(correlate, spectra)
    visibility = jnp.transpose(packed_all, (1, 0, 2))
    return (visibility, beam)
```

```python
import math

import jax
import jax.numpy as jnp
from jax import lax
from jax.sharding import Mesh, PartitionSpec as P

NIN = 256
P_SIZE = 512
TAPS = 4
NCH = 128
ZG, ZQ, CORE, INP = 2, 4, 2, 32
TM = ("zg", "zq", "core")


def dft_table(chan_table):
    chosen = chan_table[:NCH]
    points = jnp.arange(P_SIZE, dtype=jnp.int32)
    phase = chosen[:, None] * points[None, :] % P_SIZE
    angle = phase.astype(jnp.float32) * (2.0 * math.pi / P_SIZE)
    factor = 1.0 / math.sqrt(P_SIZE)
    table = jnp.stack([jnp.cos(angle) * factor, -jnp.sin(angle) * factor], axis=1)
    return table.astype(jnp.bfloat16)


def on_device(voltage, taps, chan_table):
    inputs_here = voltage.shape[0]
    spectra_here = voltage.shape[1] // P_SIZE
    blocks = ZG * ZQ * CORE
    volts = voltage.astype(jnp.bfloat16)
    tail = volts[:, (spectra_here - TAPS + 1) * P_SIZE :]
    earlier = lax.ppermute(tail, TM, [(i - 1, i) for i in range(1, blocks)])
    extended = jnp.concatenate([earlier, volts], axis=1).reshape(
        inputs_here, spectra_here + TAPS - 1, P_SIZE
    )
    filtered = jnp.zeros((inputs_here, spectra_here, P_SIZE), jnp.float32)
    for tap_index in range(TAPS):
        filtered = filtered + taps[tap_index] * extended[
            :, tap_index : tap_index + spectra_here, :
        ].astype(jnp.float32)
    filtered = filtered.astype(jnp.bfloat16)
    table = dft_table(chan_table).reshape(INP, ZQ, 2, P_SIZE).transpose(1, 0, 2, 3)
    table = table.reshape(ZQ * INP, 2, P_SIZE)
    spectra = jnp.einsum(
        "cqp,isp->cqis", table, filtered, preferred_element_type=jnp.float32
    ).astype(jnp.bfloat16)
    received = lax.all_to_all(spectra, ("zq", "inp"), split_axis=0, concat_axis=0, tiled=True)
    received = received.reshape(ZQ, INP, 2, inputs_here, spectra_here)
    parts = received.transpose(2, 0, 1, 3, 4).reshape(2, ZQ, NIN, spectra_here)
    power = jnp.sum(jnp.square(parts.astype(jnp.float32)), axis=(0, 2)) / NIN
    here = lax.axis_index("zq")
    beam_parts = [lax.dynamic_index_in_dim(power, here, 0, keepdims=False)]
    for step in range(1, ZQ):
        mine = lax.dynamic_index_in_dim(power, (here + step) % ZQ, 0, keepdims=False)
        beam_parts.append(
            lax.ppermute(mine, "zq", [(i, (i + step) % ZQ) for i in range(ZQ)])
        )
    stacked = jnp.stack(beam_parts)
    order = (here - jnp.arange(ZQ, dtype=jnp.int32)) % ZQ
    select = (order[:, None] == jnp.arange(ZQ, dtype=jnp.int32)[None, :]).astype(jnp.float32)
    beam = jnp.sum(jnp.where(select[:, :, None] > 0, stacked[:, None, :], 0.0), axis=0)
    re_part = jnp.einsum("qzas,qzbs->ab", parts, parts, preferred_element_type=jnp.float32)
    cross = jnp.einsum("zas,zbs->ab", parts[1], parts[0], preferred_element_type=jnp.float32)
    index = jnp.arange(NIN, dtype=jnp.int32)
    upper = index[:, None] <= index[None, :]
    packed = jnp.where(upper, re_part, cross - cross.T)
    packed = packed.reshape(ZG * ZQ, CORE, NIN // blocks, NIN)
    core = lax.axis_index("core")
    keep = jnp.where(core == 0, packed[:, 0], packed[:, 1])
    give = jnp.where(core == 0, packed[:, 1], packed[:, 0])
    pair = keep + lax.ppermute(give, "core", [(0, 1), (1, 0)])
    sums = lax.all_to_all(pair, ("zg", "zq"), split_axis=0, concat_axis=0, tiled=True)
    sums = sums.reshape(ZG, ZQ, NIN // blocks, NIN)
    visibility = (sums[0] + sums[1]).transpose(1, 0, 2)
    total = spectra_here * blocks
    return (visibility / total, beam)


def solution(mesh):
    fine = Mesh(mesh.devices.reshape(ZG, ZQ, CORE, INP), TM + ("inp",))
    in_specs = (P("inp", TM), P(), P())
    out_specs = (P(TM, "inp", None), P("inp", TM))
    return jax.shard_map(
        on_device, mesh=fine, in_specs=in_specs, out_specs=out_specs, check_vma=False
    )
```

```python
import math

import jax
import jax.numpy as jnp
from jax import lax
from jax.experimental import pallas as pl
from jax.experimental.pallas import tpu as pltpu
from jax.sharding import PartitionSpec as P

NIN = 256
P_SIZE = 512
TAPS = 4
NCH = 128
ZLO, ZQ, INP = 8, 4, 32
TM = 2 * ZLO
GROUP = ZQ * INP
MESH = pl.DeviceIdType.MESH
CHUNKS = 4


def dft_table(chan_table):
    chosen = chan_table[:NCH].reshape(INP, ZQ).T.reshape(NCH)
    points = jnp.arange(P_SIZE, dtype=jnp.int32)
    phase = chosen[:, None] * points[None, :] % P_SIZE
    angle = phase.astype(jnp.float32) * (2.0 * math.pi / P_SIZE)
    factor = 1.0 / math.sqrt(P_SIZE)
    table = jnp.stack([jnp.cos(angle) * factor, -jnp.sin(angle) * factor], axis=1)
    return table.astype(jnp.bfloat16).reshape(2 * NCH, P_SIZE)


def kernel(volt_hbm, early_ref, taps_ref, table_ref, vis_ref, beam_ref,
           volt, filt, wide, send, recv, packed, pair, sums, fin, power, beams,
           load_sem, own_sem, send_sem, recv_sem, pair_send, pair_recv,
           fin_send, fin_recv, beam_send, beam_recv):
    tm, inp = lax.axis_index("tm"), lax.axis_index("inp")
    core, zlo = tm % 2, tm // 2
    zg, zq = zlo // ZQ, zlo % ZQ
    x, y, zh = inp // 8, (inp // 2) % 4, inp % 2
    width = volt.shape[1] // CHUNKS
    spectra = volt.shape[1] // P_SIZE

    loads = [
        pltpu.make_async_copy(
            volt_hbm.at[:, pl.ds(n * width, width)],
            volt.at[:, pl.ds(n * width, width)],
            load_sem.at[n],
        )
        for n in range(CHUNKS)
    ]
    for load in loads:
        load.start()

    def member(step):
        q = (zq + step // INP) % ZQ
        across = (x + (step // 2) % 4) % 4
        up = (y + (step // 8) % 4) % 4
        return q, (across * 4 + up) * 2 + (zh + step % 2) % 2

    def device(q, other):
        return ((zg * ZQ + q) * 2 + core, other)

    barrier = pltpu.get_barrier_semaphore()

    @pl.loop(1, GROUP)
    def _(step):
        pl.semaphore_signal(barrier, inc=1, device_id=device(*member(step)), device_id_type=MESH)

    for q in range(ZQ):
        pl.semaphore_signal(
            barrier, inc=1, device_id=(((1 - zg) * ZQ + q) * 2 + core, inp), device_id_type=MESH
        )
    pl.semaphore_signal(barrier, inc=1, device_id=(zlo * 2 + 1 - core, inp), device_id_type=MESH)

    coef = [jnp.broadcast_to(taps_ref[k : k + 1, :], (8, P_SIZE)) for k in range(TAPS)]
    early = early_ref[...].astype(jnp.float32)
    window = tuple(early[:, k * P_SIZE : (k + 1) * P_SIZE] for k in range(TAPS - 1))
    unroll = 8

    def filter_step(it, held):
        for u in range(unroll):
            s = it * unroll + u
            start = pl.multiple_of(s * P_SIZE, P_SIZE)
            now = volt[:, pl.ds(start, P_SIZE)].astype(jnp.float32)
            total = coef[0] * held[0]
            total = total + coef[1] * held[1]
            total = total + coef[2] * held[2]
            total = total + coef[3] * now
            row = pl.multiple_of(s * 8, 8)
            for lane in range(P_SIZE // 128):
                filt[lane, pl.ds(row, 8), :] = total[:, lane * 128 : (lane + 1) * 128]
            held = (held[1], held[2], now)
        return held

    steps = spectra // CHUNKS // unroll
    for n in range(CHUNKS):
        loads[n].wait()
        window = lax.fori_loop(n * steps, (n + 1) * steps, filter_step, window)

    table = table_ref[...]
    for i in range(8):
        block = jnp.concatenate(
            [filt[lane, pl.ds(i, spectra, stride=8), :] for lane in range(P_SIZE // 128)], axis=1
        ).astype(jnp.bfloat16)
        out = lax.dot_general(
            table, block, (((1,), (1,)), ((), ())), preferred_element_type=jnp.float32
        )
        for lane in range(spectra // 128):
            wide[lane, pl.ds(i, 2 * NCH, stride=8), :] = out[:, lane * 128 : (lane + 1) * 128]

    @pl.loop(0, 16)
    def _(it):
        rows = pl.ds(pl.multiple_of(it * 128, 128), 128)
        for lane in range(spectra // 128):
            part = wide[lane, rows, :].astype(jnp.bfloat16)
            send[pl.ds(it * 8, 8), :, :, lane * 128 : (lane + 1) * 128] = part.reshape(8, 2, 8, 128)

    mine = zq * INP + inp
    pl.semaphore_wait(barrier, GROUP - 1 + ZQ + 1)

    own = pltpu.make_async_copy(send.at[mine], recv.at[mine], own_sem)
    own.start()

    @pl.loop(1, GROUP)
    def _(step):
        q, other = member(step)
        pltpu.make_async_remote_copy(
            send.at[q * INP + other], recv.at[mine], send_sem, recv_sem,
            device_id=device(q, other), device_id_type=MESH,
        ).start()

    own.wait()
    every = recv.at[pl.ds(0, GROUP - 1)]
    pltpu.make_async_copy(every, every, recv_sem).wait()

    real = jnp.zeros((NIN, NIN), jnp.float32)
    cross = jnp.zeros((NIN, NIN), jnp.float32)
    nt = (((1,), (1,)), ((), ()))
    for z in range(ZQ):
        re = recv[z * INP : (z + 1) * INP, 0].reshape(NIN, spectra)
        im = recv[z * INP : (z + 1) * INP, 1].reshape(NIN, spectra)
        both = jnp.concatenate([re, im], axis=1)
        real += lax.dot_general(both, both, nt, preferred_element_type=jnp.float32)
        cross += lax.dot_general(im, re, nt, preferred_element_type=jnp.float32)
    row = lax.broadcasted_iota(jnp.int32, (NIN, NIN), 0)
    col = lax.broadcasted_iota(jnp.int32, (NIN, NIN), 1)
    result = jnp.where(row <= col, real, cross - cross.T) * (1.0 / (spectra * TM))
    result = result.reshape(ZLO, 2, NIN // TM, NIN)
    packed[0] = result[:, 0]
    packed[1] = result[:, 1]

    swap = pltpu.make_async_remote_copy(
        packed.at[1 - core], pair, pair_send, pair_recv,
        device_id=(zlo * 2 + 1 - core, inp), device_id_type=MESH,
    )
    swap.start()

    for z in range(ZQ):
        value = recv[z * INP : (z + 1) * INP].astype(jnp.float32)
        value = jnp.sum((value * value).reshape(INP * 2, 8, spectra), axis=0)
        power[z] = jnp.sum(value, axis=0, keepdims=True) * (1.0 / NIN)
    for step in range(1, ZQ):
        q = (zq + step) % ZQ
        pltpu.make_async_remote_copy(
            power.at[q], beams.at[zq], beam_send, beam_recv,
            device_id=device(q, inp), device_id_type=MESH,
        ).start()
    beams[zq] = power[zq]

    swap.wait()
    sums[...] = packed[core] + pair[...]
    for step in range(1, ZLO):
        z = (zlo + step) % ZLO
        pltpu.make_async_remote_copy(
            sums.at[z], fin.at[zlo], fin_send, fin_recv,
            device_id=(z * 2 + core, inp), device_id_type=MESH,
        ).start()
    fin[zlo] = sums[zlo]
    three = beams.at[pl.ds(0, ZQ - 1)]
    pltpu.make_async_copy(three, three, beam_recv).wait()
    seven = fin.at[pl.ds(0, ZLO - 1)]
    pltpu.make_async_copy(seven, seven, fin_recv).wait()
    beam_ref[...] = beams[...]
    vis_ref[...] = fin[0:ZQ] + fin[ZQ:ZLO]
    pltpu.make_async_copy(every, every, send_sem).wait()
    pltpu.make_async_copy(three, three, beam_send).wait()
    pltpu.make_async_copy(seven, seven, fin_send).wait()


def on_device(voltage, taps, chan_table):
    inputs_here, samples = voltage.shape
    spectra = samples // P_SIZE
    tail = voltage[:, (spectra - TAPS + 1) * P_SIZE :].astype(jnp.bfloat16)
    early = lax.ppermute(tail, "tm", [(i - 1, i) for i in range(1, TM)])
    table = dft_table(chan_table)
    vmem = pl.BlockSpec(memory_space=pltpu.VMEM)
    rows = NIN // TM
    f32, bf16 = jnp.float32, jnp.bfloat16
    dma = pltpu.SemaphoreType.DMA
    vis, beam = pl.pallas_call(
        kernel,
        out_shape=(
            jax.ShapeDtypeStruct((ZQ, rows, NIN), f32),
            jax.ShapeDtypeStruct((ZQ, 1, spectra), f32),
        ),
        in_specs=[pl.BlockSpec(memory_space=pl.ANY), vmem, vmem, vmem],
        out_specs=(vmem, vmem),
        scratch_shapes=[
            pltpu.VMEM((inputs_here, samples), jnp.int32),
            pltpu.VMEM((P_SIZE // 128, spectra * 8, 128), f32),
            pltpu.VMEM((spectra // 128, 2 * NCH * 8, 128), f32),
            pltpu.VMEM((GROUP, 2, 8, spectra), bf16),
            pltpu.VMEM((GROUP, 2, 8, spectra), bf16),
            pltpu.VMEM((2, ZLO, rows, NIN), f32),
            pltpu.VMEM((ZLO, rows, NIN), f32),
            pltpu.VMEM((ZLO, rows, NIN), f32),
            pltpu.VMEM((ZLO, rows, NIN), f32),
            pltpu.VMEM((ZQ, 1, spectra), f32),
            pltpu.VMEM((ZQ, 1, spectra), f32),
            dma((CHUNKS,)), dma, dma, dma, dma, dma, dma, dma, dma, dma,
        ],
        compiler_params=pltpu.CompilerParams(
            collective_id=0, has_side_effects=True, vmem_limit_bytes=40 << 20
        ),
    )(voltage, early, taps, table)
    return vis.transpose(1, 0, 2), beam.reshape(ZQ, spectra)


def solution(mesh):
    in_specs = (P("inp", "tm"), P(), P())
    out_specs = (P("tm", "inp", None), P("inp", "tm"))
    return jax.shard_map(
        on_device, mesh=mesh, in_specs=in_specs, out_specs=out_specs, check_vma=False
    )
```

```python
import math

import jax
import jax.numpy as jnp
import numpy as np
from jax import lax
from jax.experimental import pallas as pl
from jax.experimental.pallas import tpu as pltpu
from jax.sharding import PartitionSpec as P

NIN = 256
P_SIZE = 512
TAPS = 4
NCH = 128
BAND = 256
ZLO, ZQ, INP = 8, 4, 32
TM = 2 * ZLO
GROUP = ZQ * INP
MESH = pl.DeviceIdType.MESH
CHUNKS = 4


def full_table():
    channel = np.arange(BAND)[:, None]
    phase = channel * np.arange(P_SIZE)[None, :] % P_SIZE
    angle = phase * (2.0 * math.pi / P_SIZE)
    factor = 1.0 / math.sqrt(P_SIZE)
    both = np.concatenate([np.cos(angle) * factor, -np.sin(angle) * factor])
    return both.astype(np.float32).astype(jnp.bfloat16)


def kernel(volt_hbm, taps_hbm, chan_hbm, full_hbm, vis_ref, beam_ref,
           volt, taps_ref, chan_ref, full_ref, tail, early, filt, wide, send, recv, packed, pair, sums, fin, power, beams,
           load_sem, taps_sem, chan_sem, full_sem, halo_send, halo_recv, own_sem, send_sem, recv_sem, pair_send, pair_recv,
           fin_send, fin_recv, beam_send, beam_recv):
    tm, inp = lax.axis_index("tm"), lax.axis_index("inp")
    core, zlo = tm % 2, tm // 2
    zg, zq = zlo // ZQ, zlo % ZQ
    x, y, zh = inp // 8, (inp // 2) % 4, inp % 2
    width = volt.shape[1] // CHUNKS
    spectra = volt.shape[1] // P_SIZE

    loads = [
        pltpu.make_async_copy(
            volt_hbm.at[:, pl.ds(n * width, width)],
            volt.at[:, pl.ds(n * width, width)],
            load_sem.at[n],
        )
        for n in range(CHUNKS)
    ]
    chan_load = pltpu.make_async_copy(chan_hbm, chan_ref, chan_sem)
    full_load = pltpu.make_async_copy(full_hbm, full_ref, full_sem)
    taps_load = pltpu.make_async_copy(taps_hbm, taps_ref, taps_sem)
    for load in [chan_load, taps_load, loads[0], full_load] + loads[1:]:
        load.start()

    def member(step):
        q = (zq + step // INP) % ZQ
        across = (x + (step // 2) % 4) % 4
        up = (y + (step // 8) % 4) % 4
        return q, (across * 4 + up) * 2 + (zh + step % 2) % 2

    def device(q, other):
        return ((zg * ZQ + q) * 2 + core, other)

    barrier = pltpu.get_barrier_semaphore()

    def greet(step):
        pl.semaphore_signal(barrier, inc=1, device_id=device(*member(step)), device_id_type=MESH)

    @pl.loop(0, GROUP // 2)
    def _(half):
        greet(2 * half + 1)

    @pl.loop(1, GROUP // 2)
    def _(half):
        greet(2 * half)

    for q in range(ZQ):
        pl.semaphore_signal(
            barrier, inc=1, device_id=(((1 - zg) * ZQ + q) * 2 + core, inp), device_id_type=MESH
        )
    pl.semaphore_signal(barrier, inc=1, device_id=(zlo * 2 + 1 - core, inp), device_id_type=MESH)

    @pl.when(jnp.logical_and(tm > 0, tm < TM - 1))
    def _():
        pl.semaphore_signal(
            barrier, inc=1, device_id=(tm + 2 * core - 1, inp), device_id_type=MESH
        )

    chan_load.wait()
    row = lax.broadcasted_iota(jnp.int32, (2 * NCH, BAND), 0)
    slot = lax.broadcasted_iota(jnp.int32, (2 * NCH, BAND), 1)
    goes = row // 2
    wanted = slot == (goes % INP) * ZQ + goes // INP
    chan = jnp.broadcast_to(chan_ref[...], (2 * NCH, BAND)).astype(jnp.float32)
    chosen = jnp.sum(jnp.where(wanted, chan, 0.0), axis=1, keepdims=True)
    lane = lax.broadcasted_iota(jnp.int32, (2 * NCH, 2 * BAND), 1)
    part = lax.broadcasted_iota(jnp.int32, (2 * NCH, 2 * BAND), 0) % 2
    pick = (lane - part * BAND).astype(jnp.float32) == chosen
    taps_load.wait()

    coef = [jnp.broadcast_to(taps_ref[k : k + 1, :], (8, P_SIZE)) for k in range(TAPS)]
    window = (jnp.zeros((8, P_SIZE), jnp.float32),) * (TAPS - 1)
    unroll = 8

    def filter_one(s, held):
        start = pl.multiple_of(s * P_SIZE, P_SIZE)
        now = volt[:, pl.ds(start, P_SIZE)].astype(jnp.float32)
        total = coef[0] * held[0]
        total = total + coef[1] * held[1]
        total = total + coef[2] * held[2]
        total = total + coef[3] * now
        row = pl.multiple_of(s * 8, 8)
        for lane in range(P_SIZE // 128):
            filt[lane, pl.ds(row, 8), :] = total[:, lane * 128 : (lane + 1) * 128]
        return (held[1], held[2], now)

    def filter_step(it, held):
        for u in range(unroll):
            held = filter_one(it * unroll + u, held)
        return held

    steps = spectra // CHUNKS // unroll
    for n in range(CHUNKS):
        loads[n].wait()
        window = lax.fori_loop(n * steps, (n + 1) * steps, filter_step, window)
    history = (TAPS - 1) * P_SIZE
    tail[...] = volt[:, pl.ds(volt.shape[1] - history, history)].astype(jnp.float32).astype(jnp.bfloat16)

    full_load.wait()
    table = jnp.dot(
        jnp.where(pick, 1.0, 0.0).astype(jnp.bfloat16), full_ref[...],
        preferred_element_type=jnp.float32,
    ).astype(jnp.bfloat16)

    def transform(tile):
        for i in range(8):
            block = jnp.concatenate(
                [
                    filt[lane, pl.ds(tile * 1024 + i, 128, stride=8), :]
                    for lane in range(P_SIZE // 128)
                ],
                axis=1,
            ).astype(jnp.bfloat16)
            wide[pl.ds(i, 2 * NCH, stride=8), :] = lax.dot_general(
                table, block, (((1,), (1,)), ((), ())), preferred_element_type=jnp.float32
            )

        @pl.loop(0, 16)
        def _(it):
            rows = pl.ds(pl.multiple_of(it * 128, 128), 128)
            ready = wide[rows, :].astype(jnp.bfloat16)
            send[pl.ds(it * 8, 8), :, :, tile * 128 : (tile + 1) * 128] = ready.reshape(8, 2, 8, 128)

    transform(1)

    mine = zq * INP + inp

    def block_power(z):
        value = recv[pl.ds(z * INP, INP)].astype(jnp.float32)
        value = jnp.sum((value * value).reshape(INP * 2, 8, spectra), axis=0)
        power[z] = jnp.sum(value, axis=0, keepdims=True) * (1.0 / NIN)

    def beam_copy(z):
        return pltpu.make_async_remote_copy(
            power.at[z], beams.at[zq], beam_send, beam_recv,
            device_id=device(z, inp), device_id_type=MESH,
        )

    ends = 1 - (tm + TM - 1) // TM + tm // (TM - 1)
    pl.semaphore_wait(barrier, GROUP - 1 + ZQ + 2 - ends)

    halo = pltpu.make_async_remote_copy(
        tail, early, halo_send, halo_recv,
        device_id=(lax.rem(tm + 1, TM), inp), device_id_type=MESH,
    )

    @pl.when(tm < TM - 1)
    def _():
        halo.start()

    def half(step, tile):
        q, other = member(step)
        lanes = pl.ds(tile * 128, 128)
        pltpu.make_async_remote_copy(
            send.at[q * INP + other, :, :, lanes], recv.at[mine, :, :, lanes],
            send_sem, recv_sem.at[0], device_id=device(q, other), device_id_type=MESH,
        ).start()

    @pl.loop(0, INP // 2)
    def _(k):
        half(2 * k + 1, 1)

    @pl.loop(1, INP // 2)
    def _(k):
        half(2 * k, 1)

    @pl.when(tm > 0)
    def _():
        halo.wait_recv()

    @pl.when(tm == 0)
    def _():
        early[...] = jnp.zeros_like(early)

    before = early[...].astype(jnp.float32)
    window = tuple(before[:, k * P_SIZE : (k + 1) * P_SIZE] for k in range(TAPS - 1))
    for s in range(TAPS - 1):
        window = filter_one(s, window)
    transform(0)
    own = pltpu.make_async_copy(send.at[mine], recv.at[mine], own_sem)
    own.start()

    @pl.loop(0, INP // 2)
    def _(k):
        half(2 * k + 1, 0)

    @pl.loop(1, INP // 2)
    def _(k):
        half(2 * k, 0)

    for ahead in range(1, ZQ):
        @pl.loop(ahead * INP, (ahead + 1) * INP)
        def _(step):
            q, other = member(step)
            pltpu.make_async_remote_copy(
                send.at[q * INP + other], recv.at[mine], send_sem, recv_sem.at[ahead],
                device_id=device(q, other), device_id_type=MESH,
            ).start()

    real = jnp.zeros((NIN, NIN), jnp.float32)
    cross = jnp.zeros((NIN, NIN), jnp.float32)
    nt = (((1,), (1,)), ((), ()))
    own.wait()
    for ahead in range(ZQ):
        z = (zq + ZQ - ahead) % ZQ
        came = recv.at[pl.ds(0, INP - (ahead == 0))]
        pltpu.make_async_copy(came, came, recv_sem.at[ahead]).wait()
        block = pl.ds(z * INP, INP)
        re = recv[block, 0].reshape(NIN, spectra)
        im = recv[block, 1].reshape(NIN, spectra)
        both = jnp.concatenate([re, im], axis=1)
        real += lax.dot_general(both, both, nt, preferred_element_type=jnp.float32)
        cross += lax.dot_general(im, re, nt, preferred_element_type=jnp.float32)
        if ahead < ZQ - 1:
            block_power(z)
            if ahead == 0:
                beams[zq] = power[zq]
            else:
                beam_copy(z).start()
    row = lax.broadcasted_iota(jnp.int32, (NIN, NIN), 0)
    col = lax.broadcasted_iota(jnp.int32, (NIN, NIN), 1)
    result = jnp.where(row <= col, real, cross - cross.T) * (1.0 / (spectra * TM))
    result = result.reshape(ZLO, 2, NIN // TM, NIN)
    packed[0] = result[:, 0]
    packed[1] = result[:, 1]

    swap = pltpu.make_async_remote_copy(
        packed.at[1 - core], pair, pair_send, pair_recv,
        device_id=(zlo * 2 + 1 - core, inp), device_id_type=MESH,
    )
    swap.start()

    last = (zq + 1) % ZQ
    block_power(last)
    beam_copy(last).start()

    swap.wait()
    sums[...] = packed[core] + pair[...]
    order = [(1 - zg) * ZQ + (zq + k) % ZQ for k in range(ZQ)]
    order += [zg * ZQ + (zq + k) % ZQ for k in range(1, ZQ)]
    for z in order:
        pltpu.make_async_remote_copy(
            sums.at[z], fin.at[zlo], fin_send, fin_recv,
            device_id=(z * 2 + core, inp), device_id_type=MESH,
        ).start()
    fin[zlo] = sums[zlo]
    three = beams.at[pl.ds(0, ZQ - 1)]
    pltpu.make_async_copy(three, three, beam_recv).wait()
    seven = fin.at[pl.ds(0, ZLO - 1)]
    pltpu.make_async_copy(seven, seven, fin_recv).wait()
    beam_ref[...] = beams[...]
    vis_ref[...] = fin[0:ZQ] + fin[ZQ:ZLO]
    every = recv.at[pl.ds(0, GROUP - 1)]
    pltpu.make_async_copy(every, every, send_sem).wait()

    @pl.when(tm < TM - 1)
    def _():
        halo.wait_send()

    pltpu.make_async_copy(three, three, beam_send).wait()
    pltpu.make_async_copy(seven, seven, fin_send).wait()


def place(vis_ref, beam_ref, vis_out, beam_out):
    for c in range(ZQ):
        vis_out[:, c, :] = vis_ref[c]
        beam_out[c : c + 1, :] = beam_ref[c]


def on_device(voltage, taps, chan_table):
    inputs_here, samples = voltage.shape
    spectra = samples // P_SIZE
    full = jnp.asarray(full_table())
    hbm = pl.BlockSpec(memory_space=pltpu.HBM)
    vmem = pl.BlockSpec(memory_space=pltpu.VMEM)
    rows = NIN // TM
    f32, bf16 = jnp.float32, jnp.bfloat16
    dma = pltpu.SemaphoreType.DMA
    vis, beam = pl.pallas_call(
        kernel,
        out_shape=(
            jax.ShapeDtypeStruct((ZQ, rows, NIN), f32),
            jax.ShapeDtypeStruct((ZQ, 1, spectra), f32),
        ),
        in_specs=[hbm, hbm, hbm, hbm],
        out_specs=(vmem, vmem),
        scratch_shapes=[
            pltpu.VMEM((inputs_here, samples), jnp.int32),
            pltpu.VMEM((TAPS, P_SIZE), f32),
            pltpu.VMEM((1, BAND), jnp.int32),
            pltpu.VMEM((2 * BAND, P_SIZE), bf16),
            pltpu.VMEM((inputs_here, (TAPS - 1) * P_SIZE), bf16),
            pltpu.VMEM((inputs_here, (TAPS - 1) * P_SIZE), bf16),
            pltpu.VMEM((P_SIZE // 128, spectra * 8, 128), f32),
            pltpu.VMEM((2 * NCH * 8, 128), f32),
            pltpu.VMEM((GROUP, 2, 8, spectra), bf16),
            pltpu.VMEM((GROUP, 2, 8, spectra), bf16),
            pltpu.VMEM((2, ZLO, rows, NIN), f32),
            pltpu.VMEM((ZLO, rows, NIN), f32),
            pltpu.VMEM((ZLO, rows, NIN), f32),
            pltpu.VMEM((ZLO, rows, NIN), f32),
            pltpu.VMEM((ZQ, 1, spectra), f32),
            pltpu.VMEM((ZQ, 1, spectra), f32),
            dma((CHUNKS,)), dma, dma, dma, dma, dma, dma, dma, dma((ZQ,)),
            dma, dma, dma, dma, dma, dma,
        ],
        compiler_params=pltpu.CompilerParams(
            collective_id=0, has_side_effects=True, vmem_limit_bytes=40 << 20
        ),
    )(*(pltpu.with_memory_space_constraint(a, pltpu.HBM) for a in (voltage, taps, chan_table.reshape(1, BAND), full)))
    return pl.pallas_call(
        place,
        out_shape=(
            jax.ShapeDtypeStruct((rows, ZQ, NIN), f32),
            jax.ShapeDtypeStruct((ZQ, spectra), f32),
        ),
        in_specs=[vmem, vmem],
        out_specs=(vmem, vmem),
        compiler_params=pltpu.CompilerParams(vmem_limit_bytes=4 << 20),
    )(vis, beam)


def solution(mesh):
    in_specs = (P("inp", "tm"), P(), P())
    out_specs = (P("tm", "inp", None), P("inp", "tm"))
    return jax.shard_map(
        on_device, mesh=mesh, in_specs=in_specs, out_specs=out_specs, check_vma=False
    )
```

```python
import math

import jax
import jax.numpy as jnp
import numpy as np
from jax import lax
from jax.experimental import pallas as pl
from jax.experimental.pallas import tpu as pltpu
from jax.sharding import PartitionSpec as P

NIN = 256
P_SIZE = 512
TAPS = 4
NCH = 128
BAND = 256
ZLO, ZQ, INP = 8, 4, 32
TM = 2 * ZLO
GROUP = ZQ * INP
MESH = pl.DeviceIdType.MESH
CHUNKS = 4
PHASES = (0, 1, 3, 2)


def full_table():
    channel = np.arange(BAND)[:, None]
    phase = channel * np.arange(P_SIZE)[None, :] % P_SIZE
    angle = phase * (2.0 * math.pi / P_SIZE)
    factor = 1.0 / math.sqrt(P_SIZE)
    both = np.concatenate([np.cos(angle) * factor, -np.sin(angle) * factor])
    return both.astype(np.float32).astype(jnp.bfloat16)


def kernel(volt_hbm, taps_hbm, chan_hbm, full_hbm, vis_ref, beam_ref,
           volt, taps_ref, chan_ref, full_ref, tail, early, filt, wide, send, recv, packed, pair, sums, fin, power, beams,
           load_sem, taps_sem, chan_sem, full_sem, halo_send, halo_recv, own_sem, send_sem, recv_sem, pair_send, pair_recv,
           fin_send, fin_recv, beam_send, beam_recv):
    tm, inp = lax.axis_index("tm"), lax.axis_index("inp")
    core, zlo = tm % 2, tm // 2
    zg, zq = zlo // ZQ, zlo % ZQ
    x, y, zh = inp // 8, (inp // 2) % 4, inp % 2
    width = volt.shape[1] // CHUNKS
    spectra = volt.shape[1] // P_SIZE

    loads = [
        pltpu.make_async_copy(
            volt_hbm.at[:, pl.ds(n * width, width)],
            volt.at[:, pl.ds(n * width, width)],
            load_sem.at[n],
        )
        for n in range(CHUNKS)
    ]
    chan_load = pltpu.make_async_copy(chan_hbm, chan_ref, chan_sem)
    full_load = pltpu.make_async_copy(full_hbm, full_ref, full_sem)
    taps_load = pltpu.make_async_copy(taps_hbm, taps_ref, taps_sem)
    for load in [chan_load, taps_load, loads[0], full_load] + loads[1:]:
        load.start()

    def chip(phase):
        return (zq // 2 + phase // 2) % 2 * 2 + (zq + phase) % 2

    def member(phase, step):
        across = (x + (step // 2) % 4) % 4
        up = (y + (step // 8) % 4) % 4
        return chip(phase), (across * 4 + up) * 2 + (zh + step % 2) % 2

    def device(q, other):
        return ((zg * ZQ + q) * 2 + core, other)

    barrier = pltpu.get_barrier_semaphore()

    def greet(phase, step):
        pl.semaphore_signal(
            barrier, inc=1, device_id=device(*member(phase, step)), device_id_type=MESH
        )

    for phase in PHASES:
        @pl.loop(0, INP // 2)
        def _(k):
            greet(phase, 2 * k + 1)

    for phase in PHASES:
        @pl.loop(int(phase == 0), INP // 2)
        def _(k):
            greet(phase, 2 * k)

    for q in range(ZQ):
        pl.semaphore_signal(
            barrier, inc=1, device_id=(((1 - zg) * ZQ + q) * 2 + core, inp), device_id_type=MESH
        )
    pl.semaphore_signal(barrier, inc=1, device_id=(zlo * 2 + 1 - core, inp), device_id_type=MESH)

    @pl.when(jnp.logical_and(tm > 0, tm < TM - 1))
    def _():
        pl.semaphore_signal(
            barrier, inc=1, device_id=(tm + 2 * core - 1, inp), device_id_type=MESH
        )

    chan_load.wait()
    row = lax.broadcasted_iota(jnp.int32, (2 * NCH, BAND), 0)
    slot = lax.broadcasted_iota(jnp.int32, (2 * NCH, BAND), 1)
    goes = row // 2
    wanted = slot == (goes % INP) * ZQ + goes // INP
    chan = jnp.broadcast_to(chan_ref[...], (2 * NCH, BAND)).astype(jnp.float32)
    chosen = jnp.sum(jnp.where(wanted, chan, 0.0), axis=1, keepdims=True)
    lane = lax.broadcasted_iota(jnp.int32, (2 * NCH, 2 * BAND), 1)
    part = lax.broadcasted_iota(jnp.int32, (2 * NCH, 2 * BAND), 0) % 2
    pick = (lane - part * BAND).astype(jnp.float32) == chosen
    taps_load.wait()

    coef = [jnp.broadcast_to(taps_ref[k : k + 1, :], (8, P_SIZE)) for k in range(TAPS)]
    window = (jnp.zeros((8, P_SIZE), jnp.float32),) * (TAPS - 1)
    unroll = 8

    def filter_one(s, held):
        start = pl.multiple_of(s * P_SIZE, P_SIZE)
        now = volt[:, pl.ds(start, P_SIZE)].astype(jnp.float32)
        total = coef[0] * held[0]
        total = total + coef[1] * held[1]
        total = total + coef[2] * held[2]
        total = total + coef[3] * now
        row = pl.multiple_of(s * 8, 8)
        for lane in range(P_SIZE // 128):
            filt[lane, pl.ds(row, 8), :] = total[:, lane * 128 : (lane + 1) * 128]
        return (held[1], held[2], now)

    def filter_step(it, held):
        for u in range(unroll):
            held = filter_one(it * unroll + u, held)
        return held

    steps = spectra // CHUNKS // unroll
    for n in range(CHUNKS):
        loads[n].wait()
        window = lax.fori_loop(n * steps, (n + 1) * steps, filter_step, window)
    history = (TAPS - 1) * P_SIZE
    tail[...] = volt[:, pl.ds(volt.shape[1] - history, history)].astype(jnp.float32).astype(jnp.bfloat16)

    full_load.wait()
    table = jnp.dot(
        jnp.where(pick, 1.0, 0.0).astype(jnp.bfloat16), full_ref[...],
        preferred_element_type=jnp.float32,
    ).astype(jnp.bfloat16)

    def transform(tile):
        for i in range(8):
            block = jnp.concatenate(
                [
                    filt[lane, pl.ds(tile * 1024 + i, 128, stride=8), :]
                    for lane in range(P_SIZE // 128)
                ],
                axis=1,
            ).astype(jnp.bfloat16)
            wide[pl.ds(i, 2 * NCH, stride=8), :] = lax.dot_general(
                table, block, (((1,), (1,)), ((), ())), preferred_element_type=jnp.float32
            )

        @pl.loop(0, 16)
        def _(it):
            rows = pl.ds(pl.multiple_of(it * 128, 128), 128)
            ready = wide[rows, :].astype(jnp.bfloat16)
            send[pl.ds(it * 8, 8), :, :, tile * 128 : (tile + 1) * 128] = ready.reshape(8, 2, 8, 128)

    transform(1)

    mine = zq * INP + inp

    def block_power(z):
        value = recv[pl.ds(z * INP, INP)].astype(jnp.float32)
        value = jnp.sum((value * value).reshape(INP * 2, 8, spectra), axis=0)
        power[z] = jnp.sum(value, axis=0, keepdims=True) * (1.0 / NIN)

    def beam_copy(z):
        return pltpu.make_async_remote_copy(
            power.at[z], beams.at[zq], beam_send, beam_recv,
            device_id=device(z, inp), device_id_type=MESH,
        )

    ends = 1 - (tm + TM - 1) // TM + tm // (TM - 1)
    pl.semaphore_wait(barrier, GROUP - 1 + ZQ + 2 - ends)

    halo = pltpu.make_async_remote_copy(
        tail, early, halo_send, halo_recv,
        device_id=(lax.rem(tm + 1, TM), inp), device_id_type=MESH,
    )

    @pl.when(tm < TM - 1)
    def _():
        halo.start()

    def half(step, tile):
        q, other = member(0, step)
        lanes = pl.ds(tile * 128, 128)
        pltpu.make_async_remote_copy(
            send.at[q * INP + other, :, :, lanes], recv.at[mine, :, :, lanes],
            send_sem, recv_sem.at[0], device_id=device(q, other), device_id_type=MESH,
        ).start()

    @pl.loop(0, INP // 2)
    def _(k):
        half(2 * k + 1, 1)

    @pl.loop(1, INP // 2)
    def _(k):
        half(2 * k, 1)

    @pl.when(tm > 0)
    def _():
        halo.wait_recv()

    @pl.when(tm == 0)
    def _():
        early[...] = jnp.zeros_like(early)

    before = early[...].astype(jnp.float32)
    window = tuple(before[:, k * P_SIZE : (k + 1) * P_SIZE] for k in range(TAPS - 1))
    for s in range(TAPS - 1):
        window = filter_one(s, window)
    transform(0)
    own = pltpu.make_async_copy(send.at[mine], recv.at[mine], own_sem)
    own.start()

    @pl.loop(0, INP // 2)
    def _(k):
        half(2 * k + 1, 0)

    @pl.loop(1, INP // 2)
    def _(k):
        half(2 * k, 0)

    def whole(phase, step):
        q, other = member(phase, step)
        pltpu.make_async_remote_copy(
            send.at[q * INP + other], recv.at[mine], send_sem, recv_sem.at[phase],
            device_id=device(q, other), device_id_type=MESH,
        ).start()

    for phase in PHASES[1:-1]:
        @pl.loop(0, INP)
        def _(step):
            whole(phase, step)

    for far in (1, 0):
        @pl.loop(0, INP // 2)
        def _(k):
            whole(PHASES[-1], 2 * k + far)

    real = jnp.zeros((NIN, NIN), jnp.float32)
    cross = jnp.zeros((NIN, NIN), jnp.float32)
    nt = (((1,), (1,)), ((), ()))
    own.wait()
    for phase in PHASES:
        z = chip(phase)
        came = recv.at[pl.ds(0, INP - (phase == 0))]
        pltpu.make_async_copy(came, came, recv_sem.at[phase]).wait()
        block = pl.ds(z * INP, INP)
        re = recv[block, 0].reshape(NIN, spectra)
        im = recv[block, 1].reshape(NIN, spectra)
        both = jnp.concatenate([re, im], axis=1)
        real += lax.dot_general(both, both, nt, preferred_element_type=jnp.float32)
        cross += lax.dot_general(im, re, nt, preferred_element_type=jnp.float32)
        if phase != PHASES[-1]:
            block_power(z)
            if phase == 0:
                beams[zq] = power[zq]
            else:
                beam_copy(z).start()
    row = lax.broadcasted_iota(jnp.int32, (NIN, NIN), 0)
    col = lax.broadcasted_iota(jnp.int32, (NIN, NIN), 1)
    result = jnp.where(row <= col, real, cross - cross.T) * (1.0 / (spectra * TM))
    result = result.reshape(ZLO, 2, NIN // TM, NIN)
    packed[0] = result[:, 0]
    packed[1] = result[:, 1]

    halves = [pl.ds((1 - zg) * ZQ, ZQ), pl.ds(zg * ZQ, ZQ)]
    swaps = [
        pltpu.make_async_remote_copy(
            packed.at[1 - core, rows], pair.at[rows], pair_send.at[n], pair_recv.at[n],
            device_id=(zlo * 2 + 1 - core, inp), device_id_type=MESH,
        )
        for n, rows in enumerate(halves)
    ]
    for swap in swaps:
        swap.start()

    last = chip(PHASES[-1])
    block_power(last)
    beam_copy(last).start()

    def rows_to(z):
        pltpu.make_async_remote_copy(
            sums.at[z], fin.at[zlo], fin_send, fin_recv,
            device_id=(z * 2 + core, inp), device_id_type=MESH,
        ).start()

    for n, rows in enumerate(halves):
        swaps[n].wait()
        sums[rows] = packed[core, rows] + pair[rows]
        for k in range(n, ZQ):
            rows_to((zg + 1 - n) % 2 * ZQ + (zq + k) % ZQ)
    fin[zlo] = sums[zlo]
    three = beams.at[pl.ds(0, ZQ - 1)]
    pltpu.make_async_copy(three, three, beam_recv).wait()
    seven = fin.at[pl.ds(0, ZLO - 1)]
    pltpu.make_async_copy(seven, seven, fin_recv).wait()
    beam_ref[...] = beams[...]
    vis_ref[...] = fin[0:ZQ] + fin[ZQ:ZLO]
    every = recv.at[pl.ds(0, GROUP - 1)]
    pltpu.make_async_copy(every, every, send_sem).wait()

    @pl.when(tm < TM - 1)
    def _():
        halo.wait_send()

    pltpu.make_async_copy(three, three, beam_send).wait()
    pltpu.make_async_copy(seven, seven, fin_send).wait()


def place(vis_ref, beam_ref, vis_out, beam_out):
    for c in range(ZQ):
        vis_out[:, c, :] = vis_ref[c]
        beam_out[c : c + 1, :] = beam_ref[c]


def on_device(voltage, taps, chan_table):
    inputs_here, samples = voltage.shape
    spectra = samples // P_SIZE
    full = jnp.asarray(full_table())
    hbm = pl.BlockSpec(memory_space=pltpu.HBM)
    vmem = pl.BlockSpec(memory_space=pltpu.VMEM)
    rows = NIN // TM
    f32, bf16 = jnp.float32, jnp.bfloat16
    dma = pltpu.SemaphoreType.DMA
    vis, beam = pl.pallas_call(
        kernel,
        out_shape=(
            jax.ShapeDtypeStruct((ZQ, rows, NIN), f32),
            jax.ShapeDtypeStruct((ZQ, 1, spectra), f32),
        ),
        in_specs=[hbm, hbm, hbm, hbm],
        out_specs=(vmem, vmem),
        scratch_shapes=[
            pltpu.VMEM((inputs_here, samples), jnp.int32),
            pltpu.VMEM((TAPS, P_SIZE), f32),
            pltpu.VMEM((1, BAND), jnp.int32),
            pltpu.VMEM((2 * BAND, P_SIZE), bf16),
            pltpu.VMEM((inputs_here, (TAPS - 1) * P_SIZE), bf16),
            pltpu.VMEM((inputs_here, (TAPS - 1) * P_SIZE), bf16),
            pltpu.VMEM((P_SIZE // 128, spectra * 8, 128), f32),
            pltpu.VMEM((2 * NCH * 8, 128), f32),
            pltpu.VMEM((GROUP, 2, 8, spectra), bf16),
            pltpu.VMEM((GROUP, 2, 8, spectra), bf16),
            pltpu.VMEM((2, ZLO, rows, NIN), f32),
            pltpu.VMEM((ZLO, rows, NIN), f32),
            pltpu.VMEM((ZLO, rows, NIN), f32),
            pltpu.VMEM((ZLO, rows, NIN), f32),
            pltpu.VMEM((ZQ, 1, spectra), f32),
            pltpu.VMEM((ZQ, 1, spectra), f32),
            dma((CHUNKS,)), dma, dma, dma, dma, dma, dma, dma, dma((ZQ,)),
            dma((2,)), dma((2,)), dma, dma, dma, dma,
        ],
        compiler_params=pltpu.CompilerParams(
            collective_id=0, has_side_effects=True, vmem_limit_bytes=40 << 20
        ),
    )(*(pltpu.with_memory_space_constraint(a, pltpu.HBM) for a in (voltage, taps, chan_table.reshape(1, BAND), full)))
    return pl.pallas_call(
        place,
        out_shape=(
            jax.ShapeDtypeStruct((rows, ZQ, NIN), f32),
            jax.ShapeDtypeStruct((ZQ, spectra), f32),
        ),
        in_specs=[vmem, vmem],
        out_specs=(vmem, vmem),
        compiler_params=pltpu.CompilerParams(vmem_limit_bytes=4 << 20),
    )(vis, beam)


def solution(mesh):
    in_specs = (P("inp", "tm"), P(), P())
    out_specs = (P("tm", "inp", None), P("inp", "tm"))
    return jax.shard_map(
        on_device, mesh=mesh, in_specs=in_specs, out_specs=out_specs, check_vma=False
    )
```
